32 devices in a mesh: space: 16 (over z, x, core), traj: 2 (over y).
Axes of the slice: x: 2, y: 2, z: 4, core: 2. Of those that a mesh axis runs over, the one named last changes fastest.
Arguments:
- primal_init: float32 [32, 64, 96, 128], P('traj', 'space'), may hold values from -6 to 6
- adjoint_init: float32 [32, 64, 96, 128], P('traj', 'space'), may hold values from -6 to 6
- diffusion: float32 [3, 64, 96, 128], P(None, 'space'), may hold values from 0.03 to 0.15
- velocity: float32 [3, 64, 96, 128], P(None, 'space'), may hold values from -0.12 to 0.12
- sources: int32 [2, 32], P(None, 'traj'), may hold values from 0 to 786431
Outputs:
- gram: float32 [32, 32], P(None, 'traj')
The draws below stay inside these ranges and needn't reach their ends.
All inputs are finite; a program needn't handle non-finite values.
Results may differ from the reference program's by a relative error of at most 0.0003.
Values sent between devices are 32-bit elements; how exact they have to be, the bound alone decides.
A program may use at most 128 MiB of HBM per device.

```python
import math
import jax
import jax.numpy as jnp
from jax import lax

TRAJ = 32
NX = 96
NY = 128
STEPS = 4
IMPULSE = 1024
NZ = 64


def plant(entries, stream_key, smallest, largest):
    place = [jax.random.randint(jax.random.fold_in(stream_key, axis), (), 0, length) for axis, length in enumerate(entries.shape)]
    longest = entries.shape.index(max(entries.shape))
    beside = place[:longest] + [(place[longest] + 1) % entries.shape[longest]] + place[longest + 1:]
    return entries.at[tuple(place)].set(smallest).at[tuple(beside)].set(largest)


def level_of(rng, dims, shards, low, high):
    gain = 1.0
    for position, shards_of in shards:
        steps = jax.random.uniform(jax.random.fold_in(jax.random.fold_in(rng, 6), position), (shards_of,), jnp.float32, low / len(shards), high / len(shards))
        gain = gain * jnp.repeat(jnp.exp(steps), dims[position] // shards_of).reshape((-1,) + (1,) * (len(dims) - 1 - position))
    return gain


def normal_values(rng, dims, spread, limit, split=(), held_as=jnp.bfloat16):
    level = level_of(rng, dims, split, -0.22, 0.18) if split else 1.0
    entries = jax.random.normal(rng, dims, jnp.float32) * spread * level
    return jnp.minimum(jnp.maximum(entries, -limit), limit).astype(held_as)


def setup_inputs(seed: int = 0) -> dict:
    splits = jax.random.split(jax.random.key(seed), 6)
    return {
        "primal_init": normal_values(splits[0], (TRAJ, NZ, NX, NY), 1.0, 6.0, ((0, 2), (1, 16)), jnp.float32),
        "adjoint_init": normal_values(splits[1], (TRAJ, NZ, NX, NY), 1.0, 6.0, ((0, 2), (1, 16)), jnp.float32),
        "diffusion": jnp.clip(jnp.exp(math.log(0.15) - 1.609438 * jax.random.uniform(splits[2], (3, NZ, NX, NY), jnp.float32) ** level_of(splits[2], (3, NZ, NX, NY), ((1, 16),), -0.2, 0.2)), 0.03, 0.15),
        "velocity": jnp.clip(jax.random.uniform(splits[3], (3, NZ, NX, NY), jnp.float32, -0.12, 0.12) * level_of(splits[3], (3, NZ, NX, NY), ((1, 16),), -0.4, 0.0), -0.12, 0.12),
        "sources": plant(jax.random.randint(splits[4], (2, TRAJ), 0, NZ * NX * NY), jax.random.fold_in(splits[4], 1), 0, (NZ * NX * NY) - 1).astype(jnp.int32),
    }


def next_cell(values, along):
    length = values.shape[along]
    remainder = lax.slice_in_dim(values, 1, length, axis=along)
    boundary = jnp.zeros_like(lax.slice_in_dim(values, 0, 1, axis=along))
    return jnp.concatenate([remainder, boundary], axis=along)

def prev_cell(values, along):
    length = values.shape[along]
    remainder = lax.slice_in_dim(values, 0, length - 1, axis=along)
    boundary = jnp.zeros_like(lax.slice_in_dim(values, 0, 1, axis=along))
    return jnp.concatenate([boundary, remainder], axis=along)

def primal_update(current, plus_vals, minus_vals, outflow, inflow, out_below, in_below):
    summed = current
    for component in range(3):
        summed = summed + inflow[component] * plus_vals[component] - outflow[component] * current + out_below[component] * minus_vals[component] - in_below[component] * current
    return summed

def adjoint_update(current, plus_vals, minus_vals, outflow, in_below):
    summed = current
    for component in range(3):
        summed = summed + outflow[component] * (plus_vals[component] - current) + in_below[component] * (minus_vals[component] - current)
    return summed

def reference(primal_init, adjoint_init, diffusion, velocity, sources):
    outflow = diffusion + 0.5 * velocity
    inflow = diffusion - 0.5 * velocity
    out_below = [prev_cell(outflow[component], component) for component in range(3)]
    in_below = [prev_cell(inflow[component], component) for component in range(3)]
    flat_index = jnp.arange(NZ * NX * NY, dtype=jnp.int32).reshape(NZ, NX, NY)

    def run_primal(arguments):
        initial, source = arguments
        current = initial + (flat_index == source).astype(jnp.float32) * IMPULSE
        for step_index in range(STEPS):
            plus_vals = [next_cell(current, component) for component in range(3)]
            minus_vals = [prev_cell(current, component) for component in range(3)]
            current = primal_update(current, plus_vals, minus_vals, outflow, inflow, out_below, in_below)
        return current

    def run_adjoint(arguments):
        initial, source = arguments
        current = initial + (flat_index == source).astype(jnp.float32) * IMPULSE
        for step_index in range(STEPS):
            plus_vals = [next_cell(current, component) for component in range(3)]
            minus_vals = [prev_cell(current, component) for component in range(3)]
            current = adjoint_update(current, plus_vals, minus_vals, outflow, in_below)
        return current
    primal_final = lax.map(run_primal, (primal_init, sources[0]))
    adjoint_final = lax.map(run_adjoint, (adjoint_init, sources[1]))
    gram = lax.dot_general(adjoint_final.reshape(TRAJ, -1), primal_final.reshape(TRAJ, -1), (((1,), (1,)), ((), ())), precision=lax.Precision.HIGHEST, preferred_element_type=jnp.float32)
    return gram / math.sqrt(NZ * NX * NY)
```

```python
import functools
import math

import jax
import jax.numpy as jnp
from jax import lax
from jax.experimental import pallas as pl
from jax.experimental.pallas import tpu as pltpu
from jax.sharding import PartitionSpec as P

STEPS = 4
IMPULSE = 1024
GROUP = 1
CHUNKS = 2
MESH = pl.DeviceIdType.MESH


def coefficients(dv, coef, zz):
    rows, lanes = coef.shape[2:]
    row = lax.broadcasted_iota(jnp.int32, (rows, lanes), 0)
    lane = lax.broadcasted_iota(jnp.int32, (rows, lanes), 1)

    def faces(component, plane):
        d, v = dv[0, component, plane], dv[1, component, plane]
        return d + 0.5 * v, d - 0.5 * v

    out_z, in_z = faces(0, zz + 1)
    out_z_below, in_z_below = faces(0, zz)
    out_x, in_x = faces(1, zz + 1)
    out_y, in_y = faces(2, zz + 1)
    zero = jnp.zeros((rows, lanes), jnp.float32)
    below_x = lambda value: jnp.where(row == 0, zero, pltpu.roll(value, 1, 0))
    below_y = lambda value: jnp.where(lane == 0, zero, pltpu.roll(value, 1, 1))
    centre = out_z + in_z_below + out_x + below_x(in_x) + out_y + below_y(in_y)
    coef[0, zz] = 1.0 - centre
    coef[1, zz] = in_z
    coef[2, zz] = out_z_below
    coef[3, zz] = jnp.where(row == rows - 1, zero, in_x)
    coef[4, zz] = below_x(out_x)
    coef[5, zz] = jnp.where(lane == lanes - 1, zero, in_y)
    coef[6, zz] = below_y(out_y)


def kernel(
    dims,
    src_ref,
    p_ref,
    a_ref,
    d_ref,
    v_ref,
    out_ref,
    cur,
    a_all,
    dv,
    coef,
    gred,
    part,
    part2,
    local_sem,
    coef_send,
    coef_recv,
    below_send,
    below_recv,
    a_send,
    a_recv,
    up_send,
    up_recv,
    down_send,
    down_recv,
    red_send,
    red_recv,
    red2_send,
    red2_recv,
):
    n, n_traj, quad, chunks = dims
    fields, planes, rows, lanes = p_ref.shape
    size = fields // chunks
    steps = 2 * STEPS
    me = lax.axis_index("space")
    my_traj = lax.axis_index("traj")
    has_up, has_down = me < n - 1, me > 0

    barrier = pltpu.get_barrier_semaphore()

    @pl.loop(1, n)
    def _(ahead):
        pl.semaphore_signal(
            barrier, inc=1, device_id={"space": lax.rem(me + ahead, n)}, device_id_type=MESH
        )

    for ahead in range(1, n_traj):
        pl.semaphore_signal(
            barrier,
            inc=1,
            device_id={"traj": lax.rem(my_traj + ahead, n_traj)},
            device_id_type=MESH,
        )
    pl.semaphore_wait(barrier, n - 1 + n_traj - 1)

    local = [
        pltpu.make_async_copy(ref, dv.at[i, :, pl.ds(1, planes)], local_sem.at[i])
        for i, ref in enumerate((d_ref, v_ref))
    ]
    for copy in local:
        copy.start()

    def below(i, ref):
        return pltpu.make_async_remote_copy(
            src_ref=ref.at[0, planes - 1],
            dst_ref=dv.at[i, 0, 0],
            send_sem=below_send.at[i],
            recv_sem=below_recv.at[i],
            device_id={"space": jnp.minimum(me + 1, n - 1)},
            device_id_type=MESH,
        )

    @pl.when(has_up)
    def _():
        for i, ref in enumerate((d_ref, v_ref)):
            below(i, ref).start()

    grid = (rows, lanes)
    offset = lax.broadcasted_iota(jnp.int32, grid, 0) * lanes + lax.broadcasted_iota(
        jnp.int32, grid, 1
    )

    def halo_up(slot, chunk):
        which = pl.ds(chunk * size, size)
        return pltpu.make_async_remote_copy(
            src_ref=cur.at[slot, which, planes],
            dst_ref=cur.at[slot, which, 0],
            send_sem=up_send.at[slot, chunk],
            recv_sem=up_recv.at[slot, chunk],
            device_id={"space": jnp.minimum(me + 1, n - 1)},
            device_id_type=MESH,
        )

    def halo_down(slot, chunk):
        which = pl.ds(chunk * size, size)
        return pltpu.make_async_remote_copy(
            src_ref=cur.at[slot, which, 1],
            dst_ref=cur.at[slot, which, planes + 1],
            send_sem=down_send.at[slot, chunk],
            recv_sem=down_recv.at[slot, chunk],
            device_id={"space": jnp.maximum(me - 1, 0)},
            device_id_type=MESH,
        )

    def send_halos(slot, chunk):
        @pl.when(has_up)
        def _():
            halo_up(slot, chunk).start()

        @pl.when(has_down)
        def _():
            halo_down(slot, chunk).start()

    def wait_sent(slot, chunk):
        @pl.when(has_up)
        def _():
            halo_up(slot, chunk).wait_send()

        @pl.when(has_down)
        def _():
            halo_down(slot, chunk).wait_send()

    def wait_halos(slot, chunk):
        @pl.when(has_down)
        def _():
            halo_up(slot, chunk).wait_recv()

        @pl.when(has_up)
        def _():
            halo_down(slot, chunk).wait_recv()

    for chunk in range(chunks):

        @pl.loop(chunk * size, (chunk + 1) * size)
        def _(f):
            source = src_ref[0, f]
            for zz in range(planes):
                cell = offset + (me * planes + zz) * (rows * lanes)
                cur[0, f, zz + 1] = p_ref[f, zz] + jnp.where(cell == source, float(IMPULSE), 0.0)

        send_halos(0, chunk)

    @pl.loop(0, fields)
    def _(f):
        source = src_ref[1, f]
        for zz in range(planes):
            cell = offset + (me * planes + zz) * (rows * lanes)
            a_all[my_traj, f, zz] = a_ref[f, zz] + jnp.where(cell == source, float(IMPULSE), 0.0)

    def gather(ahead):
        return pltpu.make_async_remote_copy(
            src_ref=a_all.at[my_traj],
            dst_ref=a_all.at[my_traj],
            send_sem=a_send.at[ahead - 1],
            recv_sem=a_recv.at[ahead - 1],
            device_id={"traj": lax.rem(my_traj + ahead, n_traj)},
            device_id_type=MESH,
        )

    for ahead in range(1, n_traj):
        gather(ahead).start()

    @pl.when(me == 0)
    def _():
        dv[:, 0, 0] = jnp.zeros((2, rows, lanes), jnp.float32)

        @pl.loop(0, fields)
        def _(f):
            for slot in range(2):
                cur[slot, f, 0] = jnp.zeros(grid, jnp.float32)

    @pl.when(me == n - 1)
    def _():
        @pl.loop(0, fields)
        def _(f):
            for slot in range(2):
                cur[slot, f, planes + 1] = jnp.zeros(grid, jnp.float32)

    for copy in local:
        copy.wait()

    @pl.when(has_down)
    def _():
        for i, ref in enumerate((d_ref, v_ref)):
            below(i, ref).wait_recv()

    @pl.loop(0, planes)
    def _(zz):
        coefficients(dv, coef, zz)

    def update(slot, f, zz):
        p = cur[slot, f, zz + 1]
        cur[1 - slot, f, zz + 1] = (
            coef[0, zz] * p
            + coef[1, zz] * cur[slot, f, zz + 2]
            + coef[2, zz] * cur[slot, f, zz]
            + coef[3, zz] * pltpu.roll(p, rows - 1, 0)
            + coef[4, zz] * pltpu.roll(p, 1, 0)
            + coef[5, zz] * pltpu.roll(p, lanes - 1, 1)
            + coef[6, zz] * pltpu.roll(p, 1, 1)
        )

    def outer_planes(slot, chunk):
        @pl.loop(chunk * size, (chunk + 1) * size)
        def _(f):
            for zz in (0, planes - 1):
                update(slot, f, zz)

    def inner_planes(slot, chunk):
        @pl.loop(chunk * size, (chunk + 1) * size)
        def _(f):
            for zz in range(1, planes - 1):
                update(slot, f, zz)

    @pl.loop(0, steps - 1)
    def _(t):
        slot = lax.rem(t, 2)
        for chunk in range(chunks):

            @pl.when(t > 0)
            def _():
                wait_sent(1 - slot, chunk)

            wait_halos(slot, chunk)
            outer_planes(slot, chunk)
            send_halos(1 - slot, chunk)
            inner_planes(slot, chunk)

    side = math.gcd(4, size)
    total = n_traj * fields

    def gram_of(chunk):
        tiles = rows // 8

        @pl.loop(0, total // 4)
        def _(kb):
            owner, k0 = lax.div(kb * 4, fields), lax.rem(kb * 4, fields)

            @pl.loop(0, size // side)
            def _(jb):
                j0 = chunk * size + jb * side

                def tile(i, sums):
                    zz, start = lax.div(i, tiles), pl.multiple_of(lax.rem(i, tiles) * 8, 8)
                    left = [a_all[owner, k0 + k, zz, pl.ds(start, 8)] for k in range(4)]
                    right = [cur[0, j0 + j, zz + 1, pl.ds(start, 8)] for j in range(side)]
                    return tuple(
                        sums[k * side + j] + left[k] * right[j]
                        for k in range(4)
                        for j in range(side)
                    )

                zero = jnp.zeros((8, lanes), jnp.float32)
                sums = lax.fori_loop(0, planes * tiles, tile, (zero,) * (4 * side), unroll=4)
                for k in range(4):
                    for j in range(side):
                        gred[kb * 4 + k, pl.ds(j0 + j, 1)] = jnp.sum(
                            sums[k * side + j], axis=0, keepdims=True
                        )

    for chunk in range(chunks):
        wait_sent(0, chunk)
        wait_halos(1, chunk)
        outer_planes(1, chunk)
        inner_planes(1, chunk)
        if chunk == 0:
            for ahead in range(1, n_traj):
                gather(ahead).wait_recv()
        gram_of(chunk)

    for chunk in range(chunks):
        wait_sent(1, chunk)

    groups = n // quad
    mine, place = lax.div(me, quad), lax.rem(me, quad)
    part[place] = jnp.sum(gred[...], axis=-1)

    def inside(ahead):
        return pltpu.make_async_remote_copy(
            src_ref=part.at[place],
            dst_ref=part.at[place],
            send_sem=red_send.at[ahead - 1],
            recv_sem=red_recv.at[ahead - 1],
            device_id={"space": mine * quad + lax.rem(place + ahead, quad)},
            device_id_type=MESH,
        )

    for ahead in range(1, quad):
        inside(ahead).start()
    for ahead in range(1, quad):
        inside(ahead).wait_recv()
    value = part[0]
    for i in range(1, quad):
        value = value + part[i]
    part2[mine] = value

    def across(ahead):
        return pltpu.make_async_remote_copy(
            src_ref=part2.at[mine],
            dst_ref=part2.at[mine],
            send_sem=red2_send.at[ahead - 1],
            recv_sem=red2_recv.at[ahead - 1],
            device_id={"space": lax.rem(mine + ahead, groups) * quad + place},
            device_id_type=MESH,
        )

    for ahead in range(1, groups):
        across(ahead).start()
    for ahead in range(1, groups):
        across(ahead).wait_recv()
    value = part2[0]
    for i in range(1, groups):
        value = value + part2[i]
    out_ref[...] = value / math.sqrt(n * planes * rows * lanes)

    for ahead in range(1, quad):
        inside(ahead).wait_send()
    for ahead in range(1, groups):
        across(ahead).wait_send()
    for ahead in range(1, n_traj):
        gather(ahead).wait_send()

    @pl.when(has_up)
    def _():
        for i, ref in enumerate((d_ref, v_ref)):
            below(i, ref).wait_send()


def solution(mesh):
    n, n_traj = mesh.shape["space"], mesh.shape["traj"]

    def on_device(primal_init, adjoint_init, diffusion, velocity, sources):
        fields, planes, rows, lanes = primal_init.shape
        quad = math.gcd(4, n)
        chunks = math.gcd(CHUNKS, fields)
        total = n_traj * fields
        vmem = pl.BlockSpec(memory_space=pltpu.VMEM)
        dma = pltpu.SemaphoreType.DMA
        f32 = jnp.float32
        return pl.pallas_call(
            functools.partial(kernel, (n, n_traj, quad, chunks)),
            out_shape=jax.ShapeDtypeStruct((total, fields), f32),
            in_specs=[pl.BlockSpec(memory_space=pltpu.SMEM)] + [vmem] * 4,
            out_specs=vmem,
            scratch_shapes=[
                pltpu.VMEM((2, fields, planes + 2, rows, lanes), f32),
                pltpu.VMEM((n_traj, fields, planes, rows, lanes), f32),
                pltpu.VMEM((2, 3, planes + 1, rows, lanes), f32),
                pltpu.VMEM((7, planes, rows, lanes), f32),
                pltpu.VMEM((total, fields, lanes), f32),
                pltpu.VMEM((quad, total, fields), f32),
                pltpu.VMEM((n // quad, total, fields), f32),
                dma((2,)),
                dma((2,)),
                dma((2,)),
                dma((2,)),
                dma((2,)),
                dma((max(1, n_traj - 1),)),
                dma((max(1, n_traj - 1),)),
                dma((2, chunks)),
                dma((2, chunks)),
                dma((2, chunks)),
                dma((2, chunks)),
                dma((max(1, quad - 1),)),
                dma((max(1, quad - 1),)),
                dma((max(1, n // quad - 1),)),
                dma((max(1, n // quad - 1),)),
            ],
            compiler_params=pltpu.CompilerParams(
                collective_id=0, has_side_effects=True, vmem_limit_bytes=48 << 20
            ),
        )(sources, primal_init, adjoint_init, diffusion, velocity)

    return jax.shard_map(
        on_device,
        mesh=mesh,
        in_specs=(
            P("traj", "space", None, None),
            P("traj", "space", None, None),
            P(None, "space", None, None),
            P(None, "space", None, None),
            P(None, "traj"),
        ),
        out_specs=P(None, "traj"),
        check_vma=False,
    )
```

```python
import functools
import math

import jax
import jax.numpy as jnp
from jax import lax
from jax.experimental import pallas as pl
from jax.experimental.pallas import tpu as pltpu
from jax.sharding import PartitionSpec as P

STEPS = 4
IMPULSE = 1024
GROUP = 4
LAG = 3
MESH = pl.DeviceIdType.MESH


def coefficients(dv, coef, zz):
    rows, lanes = coef.shape[2:]
    row = lax.broadcasted_iota(jnp.int32, (rows, lanes), 0)
    lane = lax.broadcasted_iota(jnp.int32, (rows, lanes), 1)

    def faces(component, plane):
        d, v = dv[0, component, plane], dv[1, component, plane]
        return d + 0.5 * v, d - 0.5 * v

    out_z, in_z = faces(0, zz + 1)
    out_z_below, in_z_below = faces(0, zz)
    out_x, in_x = faces(1, zz + 1)
    out_y, in_y = faces(2, zz + 1)
    zero = jnp.zeros((rows, lanes), jnp.float32)
    below_x = lambda value: jnp.where(row == 0, zero, pltpu.roll(value, 1, 0))
    below_y = lambda value: jnp.where(lane == 0, zero, pltpu.roll(value, 1, 1))
    centre = out_z + in_z_below + out_x + below_x(in_x) + out_y + below_y(in_y)
    coef[0, zz] = 1.0 - centre
    coef[1, zz] = in_z
    coef[2, zz] = out_z_below
    coef[3, zz] = jnp.where(row == rows - 1, zero, in_x)
    coef[4, zz] = below_x(out_x)
    coef[5, zz] = jnp.where(lane == lanes - 1, zero, in_y)
    coef[6, zz] = below_y(out_y)


def kernel(
    dims,
    src_ref,
    p_ref,
    a_ref,
    d_ref,
    v_ref,
    out_ref,
    start,
    cur,
    final,
    a_all,
    dv,
    coef,
    gred,
    part,
    part2,
    local_sem,
    chip_send,
    chip_recv,
    far_send,
    far_recv,
    relay_send,
    relay_recv,
    below_send,
    below_recv,
    a_send,
    a_recv,
    in_send,
    in_recv,
    back_send,
    back_recv,
    up_send,
    up_recv,
    down_send,
    down_recv,
    red_send,
    red_recv,
    red2_send,
    red2_recv,
):
    n, n_traj, quad = dims
    fields, planes, rows, lanes = p_ref.shape
    held = fields // quad
    deep = planes * quad
    steps = 2 * STEPS
    me = lax.axis_index("space")
    my_traj = lax.axis_index("traj")
    groups = n // quad
    mine, place = lax.div(me, quad), lax.rem(me, quad)
    beside = place + 1 - 2 * lax.rem(place, 2)
    far = lax.rem(place + 2, quad)
    has_up, has_down = mine < groups - 1, mine > 0
    above_id = {"space": jnp.minimum(me + quad, n - quad + place)}
    below_id = {"space": jnp.maximum(me - quad, place)}

    barrier = pltpu.get_barrier_semaphore()

    @pl.loop(1, n)
    def _(ahead):
        pl.semaphore_signal(
            barrier, inc=1, device_id={"space": lax.rem(me + ahead, n)}, device_id_type=MESH
        )

    for ahead in range(1, n_traj):
        pl.semaphore_signal(
            barrier,
            inc=1,
            device_id={"traj": lax.rem(my_traj + ahead, n_traj)},
            device_id_type=MESH,
        )
    pl.semaphore_wait(barrier, n - 1 + n_traj - 1)

    pair = (d_ref, v_ref)

    def faces_at(i, piece):
        return dv.at[i, :, pl.ds(1 + planes * piece, planes)]

    def send_far(i):
        return pltpu.make_async_remote_copy(
            src_ref=pair[i],
            dst_ref=faces_at(i, place),
            send_sem=far_send.at[i],
            recv_sem=far_recv.at[i],
            device_id={"space": mine * quad + far},
            device_id_type=MESH,
        )

    def send_beside(i):
        return pltpu.make_async_remote_copy(
            src_ref=pair[i],
            dst_ref=faces_at(i, place),
            send_sem=chip_send.at[i],
            recv_sem=chip_recv.at[i],
            device_id={"space": mine * quad + beside},
            device_id_type=MESH,
        )

    def relay(i):
        return pltpu.make_async_remote_copy(
            src_ref=faces_at(i, far),
            dst_ref=faces_at(i, far),
            send_sem=relay_send.at[i],
            recv_sem=relay_recv.at[i],
            device_id={"space": mine * quad + beside},
            device_id_type=MESH,
        )

    local = [
        pltpu.make_async_copy(pair[i], faces_at(i, place), local_sem.at[i]) for i in range(2)
    ]
    for i in range(2):
        send_far(i).start()
    for i in range(2):
        send_beside(i).start()
        local[i].start()

    grid = (rows, lanes)
    offset = lax.broadcasted_iota(jnp.int32, grid, 0) * lanes + lax.broadcasted_iota(
        jnp.int32, grid, 1
    )

    def with_impulse(value, source, zz):
        cell = offset + (me * planes + zz) * (rows * lanes)
        return value + jnp.where(cell == source, float(IMPULSE), 0.0)

    def hand_over(c, ahead):
        target = lax.rem(place + ahead, quad)
        return pltpu.make_async_remote_copy(
            src_ref=start.at[target * held + c],
            dst_ref=cur.at[0, c, pl.ds(1 + planes * place, planes)],
            send_sem=in_send.at[c, ahead - 1],
            recv_sem=in_recv.at[c, ahead - 1],
            device_id={"space": mine * quad + target},
            device_id_type=MESH,
        )

    def hand_back(c, ahead):
        target = lax.rem(place + ahead, quad)
        return pltpu.make_async_remote_copy(
            src_ref=cur.at[0, c, pl.ds(1 + planes * target, planes)],
            dst_ref=final.at[place * held + c],
            send_sem=back_send.at[c, ahead - 1],
            recv_sem=back_recv.at[c, ahead - 1],
            device_id={"space": mine * quad + target},
            device_id_type=MESH,
        )

    @pl.loop(0, held)
    def _(c):
        for owner in range(quad):
            f = owner * held + c
            for zz in range(planes):
                start[f, zz] = with_impulse(p_ref[f, zz], src_ref[0, f], zz)
        for ahead in (2, 1, 3):
            hand_over(c, ahead).start()
        for zz in range(planes):
            cur[0, c, 1 + planes * place + zz] = start[place * held + c, zz]

    @pl.loop(0, fields)
    def _(f):
        for zz in range(planes):
            a_all[my_traj, f, zz] = with_impulse(a_ref[f, zz], src_ref[1, f], zz)

    def gather(ahead):
        return pltpu.make_async_remote_copy(
            src_ref=a_all.at[my_traj],
            dst_ref=a_all.at[my_traj],
            send_sem=a_send.at[ahead - 1],
            recv_sem=a_recv.at[ahead - 1],
            device_id={"traj": lax.rem(my_traj + ahead, n_traj)},
            device_id_type=MESH,
        )

    for ahead in range(1, n_traj):
        gather(ahead).start()

    @pl.when(mine == 0)
    def _():
        for i in range(2):
            dv[i, 0, 0] = jnp.zeros(grid, jnp.float32)

        @pl.loop(0, held)
        def _(c):
            for slot in range(2):
                cur[slot, c, 0] = jnp.zeros(grid, jnp.float32)

    @pl.when(mine == groups - 1)
    def _():
        @pl.loop(0, held)
        def _(c):
            for slot in range(2):
                cur[slot, c, deep + 1] = jnp.zeros(grid, jnp.float32)

    for i in range(2):
        send_far(i).wait_recv()
        relay(i).start()
    for i in range(2):
        local[i].wait()
        send_beside(i).wait_recv()
        relay(i).wait_recv()

    def below(i):
        return pltpu.make_async_remote_copy(
            src_ref=dv.at[i, 0, deep],
            dst_ref=dv.at[i, 0, 0],
            send_sem=below_send.at[i],
            recv_sem=below_recv.at[i],
            device_id=above_id,
            device_id_type=MESH,
        )

    @pl.when(has_up)
    def _():
        for i in range(2):
            below(i).start()

    @pl.loop(1, deep)
    def _(zz):
        coefficients(dv, coef, zz)

    @pl.when(has_down)
    def _():
        for i in range(2):
            below(i).wait_recv()

    coefficients(dv, coef, 0)

    def halo_up(slot, c):
        return pltpu.make_async_remote_copy(
            src_ref=cur.at[slot, c, deep],
            dst_ref=cur.at[slot, c, 0],
            send_sem=up_send.at[slot, c],
            recv_sem=up_recv.at[slot, c],
            device_id=above_id,
            device_id_type=MESH,
        )

    def halo_down(slot, c):
        return pltpu.make_async_remote_copy(
            src_ref=cur.at[slot, c, 1],
            dst_ref=cur.at[slot, c, deep + 1],
            send_sem=down_send.at[slot, c],
            recv_sem=down_recv.at[slot, c],
            device_id=below_id,
            device_id_type=MESH,
        )

    def send_halos(slot, c):
        @pl.when(has_up)
        def _():
            halo_up(slot, c).start()

        @pl.when(has_down)
        def _():
            halo_down(slot, c).start()

    def wait_sent(slot, c):
        @pl.when(has_up)
        def _():
            halo_up(slot, c).wait_send()

        @pl.when(has_down)
        def _():
            halo_down(slot, c).wait_send()

    def wait_halos(slot, c):
        @pl.when(has_down)
        def _():
            halo_up(slot, c).wait_recv()

        @pl.when(has_up)
        def _():
            halo_down(slot, c).wait_recv()

    def update(slot, c, zz):
        p = cur[slot, c, zz + 1]
        cur[1 - slot, c, zz + 1] = (
            coef[0, zz] * p
            + coef[1, zz] * cur[slot, c, zz + 2]
            + coef[2, zz] * cur[slot, c, zz]
            + coef[3, zz] * pltpu.roll(p, rows - 1, 0)
            + coef[4, zz] * pltpu.roll(p, 1, 0)
            + coef[5, zz] * pltpu.roll(p, lanes - 1, 1)
            + coef[6, zz] * pltpu.roll(p, 1, 1)
        )

    @pl.loop(0, steps + 1 + (held - 1) * LAG)
    def _(turn):
        @pl.loop(0, held)
        def _(c):
            t = turn - c * LAG - 1

            @pl.when(t == -1)
            def _():
                for ahead in range(1, quad):
                    hand_over(c, ahead).wait_recv()
                send_halos(0, c)

            @pl.when((t >= 0) & (t < steps))
            def _():
                slot = lax.rem(t, 2)

                @pl.when(t > 0)
                def _():
                    wait_sent(1 - slot, c)

                wait_halos(slot, c)
                update(slot, c, 0)
                update(slot, c, deep - 1)

                @pl.when(t < steps - 1)
                def _():
                    send_halos(1 - slot, c)

                @pl.loop(1, deep - 1)
                def _(zz):
                    update(slot, c, zz)

            @pl.when(t == steps - 1)
            def _():
                for ahead in (2, 1, 3):
                    hand_back(c, ahead).start()
                for zz in range(planes):
                    final[place * held + c, zz] = cur[0, c, 1 + planes * place + zz]

    def gram_of(c, owner):
        tiles = rows // 8

        @pl.loop(0, fields // 4)
        def _(kb):
            def tile(i, sums):
                zz, first = lax.div(i, tiles), pl.multiple_of(lax.rem(i, tiles) * 8, 8)
                left = [a_all[owner, kb * 4 + k, zz, pl.ds(first, 8)] for k in range(4)]
                right = [final[j * held + c, zz, pl.ds(first, 8)] for j in range(quad)]
                return tuple(
                    sums[k * quad + j] + left[k] * right[j] for k in range(4) for j in range(quad)
                )

            zero = jnp.zeros((8, lanes), jnp.float32)
            sums = lax.fori_loop(0, planes * tiles, tile, (zero,) * (4 * quad), unroll=4)
            for k in range(4):
                for j in range(quad):
                    gred[owner * fields + kb * 4 + k, pl.ds(j * held + c, 1)] = jnp.sum(
                        sums[k * quad + j], axis=0, keepdims=True
                    )

    for ahead in range(1, n_traj):
        gather(ahead).wait_recv()

    @pl.loop(0, held)
    def _(c):
        for ahead in range(1, quad):
            hand_back(c, ahead).wait_recv()

        @pl.loop(0, n_traj)
        def _(owner):
            gram_of(c, owner)

    @pl.loop(0, held)
    def _(c):
        wait_sent(1, c)
        for ahead in range(1, quad):
            hand_over(c, ahead).wait_send()
            hand_back(c, ahead).wait_send()

    part[place] = jnp.sum(gred[...], axis=-1)

    def inside(ahead):
        return pltpu.make_async_remote_copy(
            src_ref=part.at[place],
            dst_ref=part.at[place],
            send_sem=red_send.at[ahead - 1],
            recv_sem=red_recv.at[ahead - 1],
            device_id={"space": mine * quad + lax.rem(place + ahead, quad)},
            device_id_type=MESH,
        )

    for ahead in range(1, quad):
        inside(ahead).start()
    for ahead in range(1, quad):
        inside(ahead).wait_recv()
    value = part[0]
    for i in range(1, quad):
        value = value + part[i]
    part2[mine] = value

    def across(ahead):
        return pltpu.make_async_remote_copy(
            src_ref=part2.at[mine],
            dst_ref=part2.at[mine],
            send_sem=red2_send.at[ahead - 1],
            recv_sem=red2_recv.at[ahead - 1],
            device_id={"space": lax.rem(mine + ahead, groups) * quad + place},
            device_id_type=MESH,
        )

    for ahead in range(1, groups):
        across(ahead).start()
    for ahead in range(1, groups):
        across(ahead).wait_recv()
    value = part2[0]
    for i in range(1, groups):
        value = value + part2[i]
    out_ref[...] = value / math.sqrt(n * planes * rows * lanes)

    for ahead in range(1, quad):
        inside(ahead).wait_send()
    for ahead in range(1, groups):
        across(ahead).wait_send()
    for ahead in range(1, n_traj):
        gather(ahead).wait_send()

    for i in range(2):
        send_far(i).wait_send()
        send_beside(i).wait_send()
        relay(i).wait_send()

    @pl.when(has_up)
    def _():
        for i in range(2):
            below(i).wait_send()


def solution(mesh):
    n, n_traj = mesh.shape["space"], mesh.shape["traj"]

    def on_device(primal_init, adjoint_init, diffusion, velocity, sources):
        fields, planes, rows, lanes = primal_init.shape
        quad = GROUP
        assert n % quad == 0 and fields % quad == 0
        held, deep = fields // quad, planes * quad
        total = n_traj * fields
        vmem = pl.BlockSpec(memory_space=pltpu.VMEM)
        dma = pltpu.SemaphoreType.DMA
        f32 = jnp.float32
        return pl.pallas_call(
            functools.partial(kernel, (n, n_traj, quad)),
            out_shape=jax.ShapeDtypeStruct((total, fields), f32),
            in_specs=[pl.BlockSpec(memory_space=pltpu.SMEM)] + [vmem] * 4,
            out_specs=vmem,
            scratch_shapes=[
                pltpu.VMEM((fields, planes, rows, lanes), f32),
                pltpu.VMEM((2, held, deep + 2, rows, lanes), f32),
                pltpu.VMEM((fields, planes, rows, lanes), f32),
                pltpu.VMEM((n_traj, fields, planes, rows, lanes), f32),
                pltpu.VMEM((2, 3, deep + 1, rows, lanes), f32),
                pltpu.VMEM((7, deep, rows, lanes), f32),
                pltpu.VMEM((total, fields, lanes), f32),
                pltpu.VMEM((quad, total, fields), f32),
                pltpu.VMEM((n // quad, total, fields), f32),
                *[dma((2,))] * 9,
                *[dma((max(1, n_traj - 1),))] * 2,
                *[dma((held, quad - 1))] * 4,
                *[dma((2, held))] * 4,
                *[dma((quad - 1,))] * 2,
                *[dma((max(1, n // quad - 1),))] * 2,
            ],
            compiler_params=pltpu.CompilerParams(
                collective_id=0, has_side_effects=True, vmem_limit_bytes=48 << 20
            ),
        )(sources, primal_init, adjoint_init, diffusion, velocity)

    return jax.shard_map(
        on_device,
        mesh=mesh,
        in_specs=(
            P("traj", "space", None, None),
            P("traj", "space", None, None),
            P(None, "space", None, None),
            P(None, "space", None, None),
            P(None, "traj"),
        ),
        out_specs=P(None, "traj"),
        check_vma=False,
    )
```

```python
import functools
import math

import jax
import jax.numpy as jnp
from jax import lax
from jax.experimental import pallas as pl
from jax.experimental.pallas import tpu as pltpu
from jax.sharding import PartitionSpec as P

STEPS = 4
IMPULSE = 1024
GROUP = 4
LAG = 2
MESH = pl.DeviceIdType.MESH


def coefficients(dv, coef, zz):
    rows, lanes = coef.shape[2:]
    row = lax.broadcasted_iota(jnp.int32, (rows, lanes), 0)
    lane = lax.broadcasted_iota(jnp.int32, (rows, lanes), 1)

    def faces(component, plane):
        d, v = dv[0, component, plane], dv[1, component, plane]
        return d + 0.5 * v, d - 0.5 * v

    out_z, in_z = faces(0, zz + 1)
    out_z_below, in_z_below = faces(0, zz)
    out_x, in_x = faces(1, zz + 1)
    out_y, in_y = faces(2, zz + 1)
    zero = jnp.zeros((rows, lanes), jnp.float32)
    below_x = lambda value: jnp.where(row == 0, zero, pltpu.roll(value, 1, 0))
    below_y = lambda value: jnp.where(lane == 0, zero, pltpu.roll(value, 1, 1))
    centre = out_z + in_z_below + out_x + below_x(in_x) + out_y + below_y(in_y)
    coef[0, zz] = 1.0 - centre
    coef[1, zz] = in_z
    coef[2, zz] = out_z_below
    coef[3, zz] = jnp.where(row == rows - 1, zero, in_x)
    coef[4, zz] = below_x(out_x)
    coef[5, zz] = jnp.where(lane == lanes - 1, zero, in_y)
    coef[6, zz] = below_y(out_y)


def kernel(
    dims,
    src_ref,
    p_ref,
    a_ref,
    d_ref,
    v_ref,
    out_ref,
    start,
    cur,
    final,
    a_all,
    dv,
    coef,
    gred,
    part,
    part2,
    local_sem,
    chip_send,
    chip_recv,
    far_send,
    far_recv,
    relay_send,
    relay_recv,
    below_send,
    below_recv,
    a_send,
    a_recv,
    in_send,
    in_recv,
    back_send,
    back_recv,
    up_send,
    up_recv,
    down_send,
    down_recv,
    red_send,
    red_recv,
    red2_send,
    red2_recv,
):
    n, n_traj, quad = dims
    fields, planes, rows, lanes = p_ref.shape
    held = fields // quad
    deep = planes * quad
    steps = 2 * STEPS
    me = lax.axis_index("space")
    my_traj = lax.axis_index("traj")
    groups = n // quad
    mine, place = lax.div(me, quad), lax.rem(me, quad)
    beside = place + 1 - 2 * lax.rem(place, 2)
    far = lax.rem(place + 2, quad)
    has_up, has_down = mine < groups - 1, mine > 0
    above_id = {"space": jnp.minimum(me + quad, n - quad + place)}
    below_id = {"space": jnp.maximum(me - quad, place)}

    barrier = pltpu.get_barrier_semaphore()

    @pl.loop(1, n)
    def _(ahead):
        pl.semaphore_signal(
            barrier, inc=1, device_id={"space": lax.rem(me + ahead, n)}, device_id_type=MESH
        )

    for ahead in range(1, n_traj):
        pl.semaphore_signal(
            barrier,
            inc=1,
            device_id={"traj": lax.rem(my_traj + ahead, n_traj)},
            device_id_type=MESH,
        )
    pl.semaphore_wait(barrier, n - 1 + n_traj - 1)

    pair = (d_ref, v_ref)

    def faces_at(i, piece):
        return dv.at[i, :, pl.ds(1 + planes * piece, planes)]

    def send_far(i):
        return pltpu.make_async_remote_copy(
            src_ref=pair[i],
            dst_ref=faces_at(i, place),
            send_sem=far_send.at[i],
            recv_sem=far_recv.at[i],
            device_id={"space": mine * quad + far},
            device_id_type=MESH,
        )

    def send_beside(i):
        return pltpu.make_async_remote_copy(
            src_ref=pair[i],
            dst_ref=faces_at(i, place),
            send_sem=chip_send.at[i],
            recv_sem=chip_recv.at[i],
            device_id={"space": mine * quad + beside},
            device_id_type=MESH,
        )

    def relay(i):
        return pltpu.make_async_remote_copy(
            src_ref=faces_at(i, far),
            dst_ref=faces_at(i, far),
            send_sem=relay_send.at[i],
            recv_sem=relay_recv.at[i],
            device_id={"space": mine * quad + beside},
            device_id_type=MESH,
        )

    local = [
        pltpu.make_async_copy(pair[i], faces_at(i, place), local_sem.at[i]) for i in range(2)
    ]
    for i in range(2):
        send_far(i).start()
    for i in range(2):
        send_beside(i).start()
        local[i].start()

    grid = (rows, lanes)
    offset = lax.broadcasted_iota(jnp.int32, grid, 0) * lanes + lax.broadcasted_iota(
        jnp.int32, grid, 1
    )

    def with_impulse(value, source, zz):
        cell = offset + (me * planes + zz) * (rows * lanes)
        return value + jnp.where(cell == source, float(IMPULSE), 0.0)

    def hand_over(c, ahead):
        target = lax.rem(place + ahead, quad)
        return pltpu.make_async_remote_copy(
            src_ref=start.at[target * held + c],
            dst_ref=cur.at[0, c, pl.ds(1 + planes * place, planes)],
            send_sem=in_send.at[c, ahead - 1],
            recv_sem=in_recv.at[c, ahead - 1],
            device_id={"space": mine * quad + target},
            device_id_type=MESH,
        )

    def hand_back(c, ahead):
        target = lax.rem(place + ahead, quad)
        return pltpu.make_async_remote_copy(
            src_ref=cur.at[0, c, pl.ds(1 + planes * target, planes)],
            dst_ref=final.at[place * held + c],
            send_sem=back_send.at[c, ahead - 1],
            recv_sem=back_recv.at[c, ahead - 1],
            device_id={"space": mine * quad + target},
            device_id_type=MESH,
        )

    @pl.loop(0, held)
    def _(c):
        for owner in range(quad):
            f = owner * held + c
            for zz in range(planes):
                start[f, zz] = with_impulse(p_ref[f, zz], src_ref[0, f], zz)
        for ahead in (2, 1, 3):
            hand_over(c, ahead).start()
        for zz in range(planes):
            cur[0, c, 1 + planes * place + zz] = start[place * held + c, zz]

    @pl.loop(0, fields)
    def _(f):
        for zz in range(planes):
            a_all[my_traj, f, zz] = with_impulse(a_ref[f, zz], src_ref[1, f], zz)

    def gather(ahead):
        return pltpu.make_async_remote_copy(
            src_ref=a_all.at[my_traj],
            dst_ref=a_all.at[my_traj],
            send_sem=a_send.at[ahead - 1],
            recv_sem=a_recv.at[ahead - 1],
            device_id={"traj": lax.rem(my_traj + ahead, n_traj)},
            device_id_type=MESH,
        )

    for ahead in range(1, n_traj):
        gather(ahead).start()

    @pl.when(mine == 0)
    def _():
        for i in range(2):
            dv[i, 0, 0] = jnp.zeros(grid, jnp.float32)

        @pl.loop(0, held)
        def _(c):
            for slot in range(2):
                cur[slot, c, 0] = jnp.zeros(grid, jnp.float32)

    @pl.when(mine == groups - 1)
    def _():
        @pl.loop(0, held)
        def _(c):
            for slot in range(2):
                cur[slot, c, deep + 1] = jnp.zeros(grid, jnp.float32)

    for i in range(2):
        send_far(i).wait_recv()
        relay(i).start()
    for i in range(2):
        local[i].wait()
        send_beside(i).wait_recv()
        relay(i).wait_recv()

    def below(i):
        return pltpu.make_async_remote_copy(
            src_ref=dv.at[i, 0, deep],
            dst_ref=dv.at[i, 0, 0],
            send_sem=below_send.at[i],
            recv_sem=below_recv.at[i],
            device_id=above_id,
            device_id_type=MESH,
        )

    @pl.when(has_up)
    def _():
        for i in range(2):
            below(i).start()

    @pl.loop(1, deep)
    def _(zz):
        coefficients(dv, coef, zz)

    @pl.when(has_down)
    def _():
        for i in range(2):
            below(i).wait_recv()

    coefficients(dv, coef, 0)

    def halo_up(slot, c):
        return pltpu.make_async_remote_copy(
            src_ref=cur.at[slot, c, deep],
            dst_ref=cur.at[slot, c, 0],
            send_sem=up_send.at[slot, c],
            recv_sem=up_recv.at[slot, c],
            device_id=above_id,
            device_id_type=MESH,
        )

    def halo_down(slot, c):
        return pltpu.make_async_remote_copy(
            src_ref=cur.at[slot, c, 1],
            dst_ref=cur.at[slot, c, deep + 1],
            send_sem=down_send.at[slot, c],
            recv_sem=down_recv.at[slot, c],
            device_id=below_id,
            device_id_type=MESH,
        )

    def send_halos(slot, c):
        @pl.when(has_up)
        def _():
            halo_up(slot, c).start()

        @pl.when(has_down)
        def _():
            halo_down(slot, c).start()

    def wait_sent(slot, c):
        @pl.when(has_up)
        def _():
            halo_up(slot, c).wait_send()

        @pl.when(has_down)
        def _():
            halo_down(slot, c).wait_send()

    def wait_halos(slot, c):
        @pl.when(has_down)
        def _():
            halo_up(slot, c).wait_recv()

        @pl.when(has_up)
        def _():
            halo_down(slot, c).wait_recv()

    def update(slot, c, zz):
        p = cur[slot, c, zz + 1]
        cur[1 - slot, c, zz + 1] = (
            coef[0, zz] * p
            + coef[1, zz] * cur[slot, c, zz + 2]
            + coef[2, zz] * cur[slot, c, zz]
            + coef[3, zz] * pltpu.roll(p, rows - 1, 0)
            + coef[4, zz] * pltpu.roll(p, 1, 0)
            + coef[5, zz] * pltpu.roll(p, lanes - 1, 1)
            + coef[6, zz] * pltpu.roll(p, 1, 1)
        )

    @pl.loop(0, steps + 1 + (held - 1) * LAG)
    def _(turn):
        @pl.loop(0, held)
        def _(c):
            t = turn - c * LAG - 1

            @pl.when(t == -1)
            def _():
                for ahead in range(1, quad):
                    hand_over(c, ahead).wait_recv()
                send_halos(0, c)

            @pl.when((t >= 0) & (t < steps))
            def _():
                slot = lax.rem(t, 2)

                @pl.when(t > 0)
                def _():
                    wait_sent(1 - slot, c)

                wait_halos(slot, c)
                update(slot, c, 0)
                update(slot, c, deep - 1)

                @pl.when(t < steps - 1)
                def _():
                    send_halos(1 - slot, c)

                @pl.loop(1, deep - 1)
                def _(zz):
                    update(slot, c, zz)

            @pl.when(t == steps - 1)
            def _():
                for ahead in (2, 1, 3):
                    hand_back(c, ahead).start()
                for zz in range(planes):
                    final[place * held + c, zz] = cur[0, c, 1 + planes * place + zz]

    def gram_of(c, owner):
        tiles = rows // 8

        @pl.loop(0, fields // 4)
        def _(kb):
            def tile(i, sums):
                zz, first = lax.div(i, tiles), pl.multiple_of(lax.rem(i, tiles) * 8, 8)
                left = [a_all[owner, kb * 4 + k, zz, pl.ds(first, 8)] for k in range(4)]
                right = [final[j * held + c, zz, pl.ds(first, 8)] for j in range(quad)]
                return tuple(
                    sums[k * quad + j] + left[k] * right[j] for k in range(4) for j in range(quad)
                )

            zero = jnp.zeros((8, lanes), jnp.float32)
            sums = lax.fori_loop(0, planes * tiles, tile, (zero,) * (4 * quad), unroll=4)
            for k in range(4):
                for j in range(quad):
                    gred[owner * fields + kb * 4 + k, pl.ds(j * held + c, 1)] = jnp.sum(
                        sums[k * quad + j], axis=0, keepdims=True
                    )

    for ahead in range(1, n_traj):
        gather(ahead).wait_recv()

    @pl.loop(0, held)
    def _(c):
        for ahead in range(1, quad):
            hand_back(c, ahead).wait_recv()

        @pl.loop(0, n_traj)
        def _(owner):
            gram_of(c, owner)

    @pl.loop(0, held)
    def _(c):
        wait_sent(1, c)
        for ahead in range(1, quad):
            hand_over(c, ahead).wait_send()
            hand_back(c, ahead).wait_send()

    part[place] = jnp.sum(gred[...], axis=-1)

    def inside(ahead):
        return pltpu.make_async_remote_copy(
            src_ref=part.at[place],
            dst_ref=part.at[place],
            send_sem=red_send.at[ahead - 1],
            recv_sem=red_recv.at[ahead - 1],
            device_id={"space": mine * quad + lax.rem(place + ahead, quad)},
            device_id_type=MESH,
        )

    for ahead in range(1, quad):
        inside(ahead).start()
    for ahead in range(1, quad):
        inside(ahead).wait_recv()
    value = part[0]
    for i in range(1, quad):
        value = value + part[i]
    part2[mine] = value

    def across(ahead):
        return pltpu.make_async_remote_copy(
            src_ref=part2.at[mine],
            dst_ref=part2.at[mine],
            send_sem=red2_send.at[ahead - 1],
            recv_sem=red2_recv.at[ahead - 1],
            device_id={"space": lax.rem(mine + ahead, groups) * quad + place},
            device_id_type=MESH,
        )

    for ahead in range(1, groups):
        across(ahead).start()
    for ahead in range(1, groups):
        across(ahead).wait_recv()
    value = part2[0]
    for i in range(1, groups):
        value = value + part2[i]
    out_ref[...] = value / math.sqrt(n * planes * rows * lanes)

    for ahead in range(1, quad):
        inside(ahead).wait_send()
    for ahead in range(1, groups):
        across(ahead).wait_send()
    for ahead in range(1, n_traj):
        gather(ahead).wait_send()

    for i in range(2):
        send_far(i).wait_send()
        send_beside(i).wait_send()
        relay(i).wait_send()

    @pl.when(has_up)
    def _():
        for i in range(2):
            below(i).wait_send()


def solution(mesh):
    n, n_traj = mesh.shape["space"], mesh.shape["traj"]

    def on_device(primal_init, adjoint_init, diffusion, velocity, sources):
        fields, planes, rows, lanes = primal_init.shape
        quad = GROUP
        assert n % quad == 0 and fields % quad == 0
        held, deep = fields // quad, planes * quad
        total = n_traj * fields
        vmem = pl.BlockSpec(memory_space=pltpu.VMEM)
        dma = pltpu.SemaphoreType.DMA
        f32 = jnp.float32
        return pl.pallas_call(
            functools.partial(kernel, (n, n_traj, quad)),
            out_shape=jax.ShapeDtypeStruct((total, fields), f32),
            in_specs=[pl.BlockSpec(memory_space=pltpu.SMEM)] + [vmem] * 4,
            out_specs=vmem,
            scratch_shapes=[
                pltpu.VMEM((fields, planes, rows, lanes), f32),
                pltpu.VMEM((2, held, deep + 2, rows, lanes), f32),
                pltpu.VMEM((fields, planes, rows, lanes), f32),
                pltpu.VMEM((n_traj, fields, planes, rows, lanes), f32),
                pltpu.VMEM((2, 3, deep + 1, rows, lanes), f32),
                pltpu.VMEM((7, deep, rows, lanes), f32),
                pltpu.VMEM((total, fields, lanes), f32),
                pltpu.VMEM((quad, total, fields), f32),
                pltpu.VMEM((n // quad, total, fields), f32),
                *[dma((2,))] * 9,
                *[dma((max(1, n_traj - 1),))] * 2,
                *[dma((held, quad - 1))] * 4,
                *[dma((2, held))] * 4,
                *[dma((quad - 1,))] * 2,
                *[dma((max(1, n // quad - 1),))] * 2,
            ],
            compiler_params=pltpu.CompilerParams(
                collective_id=0, has_side_effects=True, vmem_limit_bytes=48 << 20
            ),
        )(sources, primal_init, adjoint_init, diffusion, velocity)

    return jax.shard_map(
        on_device,
        mesh=mesh,
        in_specs=(
            P("traj", "space", None, None),
            P("traj", "space", None, None),
            P(None, "space", None, None),
            P(None, "space", None, None),
            P(None, "traj"),
        ),
        out_specs=P(None, "traj"),
        check_vma=False,
    )
```
